32 devices in a mesh: site: 8 (over y, x, core), scen: 4 (over z).
Axes of the slice: x: 2, y: 2, z: 4, core: 2. Of those that a mesh axis runs over, the one named last changes fastest.
Arguments:
- normals: bfloat16 [20480, 1344], P('site', 'scen'), may hold values from -6 to 6
- pattern: int32 [32, 40], replicated, may hold values from 0 to 79, as said below
- factor: bfloat16 [32, 40, 256, 256], P('site', None, 'scen'), may hold values from -0.0625 to 0.0625
- temporal: bfloat16 [168, 168], replicated, may hold values from -0.5 to 0.5
- capacity: float32 [8192], P('site'), may hold values from 0.05 to 0.4
- spread: float32 [8192], P('site'), may hold values from 0.2 to 0.8
- bus_map: int32 [8192], replicated, may hold values from 0 to 511
Outputs:
- bus_power: float32 [512, 1344], P('site', 'scen')
The draws below stay inside these ranges and needn't reach their ends.
Inputs may be any that keep to these rules, and one draw needn't show every extreme that they name: `pattern`: each block row names 40 different column blocks. The 4 block rows of one index of site (rows k * 4 to (k + 1) * 4 - 1) name at most 5 different column blocks among those held by any one index of site (blocks j * 10 to (j + 1) * 10 - 1), and exactly 5 among those held by index k itself.
All inputs are finite; a program needn't handle non-finite values.
Results may differ from the reference program's by a relative error of at most 0.0013.
Values may be sent and summed in bfloat16 or wider, within the bound.
A program may use at most 192 MiB of HBM per device.

```python
import math
import jax
import jax.numpy as jnp
from jax import lax

BLK = 256
HOURS = 168
NZ = 40
MAX_COLUMN_BLOCKS = 5
CB_DEV = 10
RB_DEV = 4
ROWS = 32
COLS = 80
SITES = 20480
SLAB = 8192
SCEN = 8
BUSES = 512


def candidate_slots(sub_key):
    return jax.random.permutation(sub_key, CB_DEV)[:MAX_COLUMN_BLOCKS].astype(jnp.int32)


def draw_pattern(key, part):
    owning_devices = ROWS // RB_DEV
    key_perm, pairing_key, key_hub, key_row = jax.random.split(jax.random.fold_in(key, 11), 4)
    local_slots = jax.vmap(candidate_slots)(jax.random.split(key_perm, owning_devices * owning_devices)).reshape(owning_devices, owning_devices, MAX_COLUMN_BLOCKS)
    holder = jnp.arange(owning_devices, dtype=jnp.int32)
    cand_columns = holder[None, :, None] * CB_DEV + local_slots
    raw_gap = jnp.abs(holder[:, None] - holder[None, :])
    block_separation = jnp.minimum(raw_gap, owning_devices - raw_gap)
    pairing_reward = jax.random.randint(pairing_key, (owning_devices, owning_devices), 0, 2048, dtype=jnp.int32) // (1 + block_separation)
    central_marker = jax.random.randint(key_hub, (owning_devices,), 0, 4, dtype=jnp.int32) == 0
    central_reward = jnp.where(central_marker, 1024, 0).astype(jnp.int32)
    ownership_reward = jnp.where(block_separation == 0, 100000, 0).astype(jnp.int32)
    device_reward = pairing_reward + central_reward[None, :] + ownership_reward
    row_holder_device = jnp.arange(ROWS, dtype=jnp.int32) // RB_DEV
    row_jitter = jax.random.randint(key_row, (ROWS, owning_devices, MAX_COLUMN_BLOCKS), 0, 1024, dtype=jnp.int32)
    tiebreak_jitter = jnp.arange(owning_devices * MAX_COLUMN_BLOCKS, dtype=jnp.int32).reshape(owning_devices, MAX_COLUMN_BLOCKS)
    placement_scores = (device_reward[row_holder_device][:, :, None] + row_jitter) * (owning_devices * MAX_COLUMN_BLOCKS) + tiebreak_jitter[None, :, :]
    chosen = lax.top_k(placement_scores.reshape(ROWS, owning_devices * MAX_COLUMN_BLOCKS), NZ)[1]
    row_cands = cand_columns[row_holder_device].reshape(ROWS, owning_devices * MAX_COLUMN_BLOCKS)
    return jnp.take_along_axis(row_cands, chosen, axis=1).astype(jnp.int32)


def touch_ends(result, stream_key, smallest, largest):
    index_at = [jax.random.randint(jax.random.fold_in(stream_key, axis), (), 0, length) for axis, length in enumerate(result.shape)]
    longest = result.shape.index(max(result.shape))
    next_to = index_at[:longest] + [(index_at[longest] + 1) % result.shape[longest]] + index_at[longest + 1:]
    return result.at[tuple(index_at)].set(smallest).at[tuple(next_to)].set(largest)


def level_of(stream_key, shape, cuts, least, high):
    gain, own = 1.0, jax.random.fold_in(stream_key, 6)
    for position, parts in cuts:
        draws = jnp.exp(jax.random.uniform(jax.random.fold_in(own, position), (parts,), jnp.float32, least / len(cuts), high / len(cuts)))
        gain = gain * jnp.repeat(draws, shape[position] // parts).reshape([-1 if axis == position else 1 for axis in range(len(shape))])
    return gain


def gaussian(own_key, dims, scale, bound, cuts=(), kind=jnp.bfloat16):
    result = scale * jax.random.normal(own_key, dims, jnp.float32)
    if cuts:
        result = result * level_of(own_key, dims, cuts, -0.22, 0.18)
    return jnp.clip(result, -bound, bound).astype(kind)


def setup_inputs(seed: int = 0) -> dict:
    splits = jax.random.split(jax.random.key(seed), 8)
    return {
        "normals": gaussian(splits[0], (SITES, SCEN * HOURS), 1.0, 6.0, ((0, 8), (1, 4))),
        "pattern": draw_pattern(jax.random.fold_in(splits[7], 71), 0),
        "factor": gaussian(splits[2], (ROWS, NZ, BLK, BLK), (NZ * BLK) ** -0.5, 0.0625, ((0, 8), (2, 4))),
        "temporal": gaussian(splits[3], (HOURS, HOURS), HOURS ** -0.5, 0.5),
        "capacity": jnp.clip(jnp.exp(math.log(0.4) - 2.0794415 * jax.random.uniform(splits[4], (SLAB,), jnp.float32) ** level_of(splits[4], (SLAB,), ((0, 8),), -0.2, 0.2)), 0.05, 0.4),
        "spread": jnp.clip(jnp.exp(math.log(0.8) - 1.3862944 * jax.random.uniform(splits[5], (SLAB,), jnp.float32) ** level_of(splits[5], (SLAB,), ((0, 8),), -0.2, 0.2)), 0.2, 0.8),
        "bus_map": touch_ends(jax.random.randint(splits[6], (SLAB,), 0, BUSES), jax.random.fold_in(splits[6], 1), 0, BUSES - 1).astype(jnp.int32),
    }


def reference(normals, pattern, factor, temporal, capacity, spread, bus_map):
    row_width = SCEN * HOURS
    blocks = normals.reshape(COLS, BLK, row_width)

    def one_block_row(inputs):
        columns, factor_row = inputs
        picked = jnp.take(blocks, columns.astype(jnp.int32), axis=0)
        spatial = jnp.einsum("tij,tjw->iw", factor_row.astype(jnp.float32), picked.astype(jnp.float32))
        return spatial.astype(jnp.bfloat16)

    spatial = lax.map(one_block_row, (pattern, factor))
    hourly = spatial.reshape(SLAB, SCEN, HOURS).astype(jnp.float32)
    weather = jnp.einsum("nsg,hg->nsh", hourly, temporal.astype(jnp.float32))
    scale_rows = capacity[:, None, None]
    spread_rows = spread[:, None, None]
    injected = (scale_rows * jnp.exp(spread_rows * weather - 0.5 * spread_rows * spread_rows)).astype(jnp.bfloat16)
    injected = injected.reshape(SLAB, row_width).astype(jnp.float32)
    return jax.ops.segment_sum(injected, bus_map.astype(jnp.int32), num_segments=BUSES)
```

```python
import jax
import jax.numpy as jnp
from jax import lax
from jax.sharding import PartitionSpec as P

BLK = 256
HOURS = 168
NZ = 40
MAX_COLUMN_BLOCKS = 5


def shards(normals, pattern, factor, temporal, capacity, spread, bus_map, buses):
    own = lax.axis_index("site")
    sites = lax.axis_size("site")
    group = lax.axis_index("scen")
    groups = lax.axis_size("scen")
    width = normals.shape[1]
    scen_here = width // HOURS
    rows_here, _, height, _ = factor.shape
    halves = groups // 2

    partner_factor = lax.ppermute(factor, "scen", [(z, z ^ 1) for z in range(groups)])
    parts = [normals]
    for s in range(1, halves):
        parts.append(
            lax.ppermute(normals, "scen", [(z, (z + 2 * s) % groups) for z in range(groups)])
        )

    block_count = normals.shape[0] // BLK
    all_blocks = block_count * sites
    block_ids = jnp.arange(all_blocks, dtype=jnp.int32)
    wanted = pattern.reshape(sites, -1)
    needed = jnp.any(wanted[:, :, None] == block_ids[None, None, :], axis=1)
    owned_need = lax.dynamic_slice_in_dim(needed, own * block_count, block_count, 1)
    owned_need = owned_need.astype(jnp.int32)
    slot_rank = jnp.cumsum(owned_need, axis=1) - 1
    slot_ids = jnp.arange(MAX_COLUMN_BLOCKS, dtype=jnp.int32)
    chosen = (owned_need[:, None, :] == 1) & (slot_rank[:, None, :] == slot_ids[None, :, None])
    local_ids = jnp.arange(block_count, dtype=jnp.int32)
    block_index = jnp.sum(jnp.where(chosen, local_ids[None, None, :], 0), axis=2)

    my_columns = lax.dynamic_slice_in_dim(pattern, own * rows_here, rows_here, 0)
    my_need = lax.dynamic_index_in_dim(needed, own, 0, keepdims=False).astype(jnp.int32)
    my_rank = (jnp.cumsum(my_need.reshape(sites, block_count), axis=1) - 1).reshape(-1)
    slot_of_block = block_ids // block_count * MAX_COLUMN_BLOCKS + my_rank
    slots = sites * MAX_COLUMN_BLOCKS
    slot_of = jnp.sum(
        jnp.where(my_columns[:, :, None] == block_ids, slot_of_block[None, None, :], 0), axis=2
    )
    match = slot_of[:, None, :] == jnp.arange(slots, dtype=jnp.int32)[None, :, None]
    place = jnp.sum(jnp.where(match, jnp.arange(NZ, dtype=jnp.int32), 0), axis=2)
    named = jnp.any(match, axis=2)

    def in_slot_order(blocks):
        flat = blocks.reshape(rows_here * NZ, height, BLK)
        index = place + jnp.arange(rows_here, dtype=jnp.int32)[:, None] * NZ
        ordered = flat[index]
        if slots > NZ:
            ordered = jnp.where(named[:, :, None, None], ordered, jnp.zeros((), flat.dtype))
        return ordered

    ordered = [in_slot_order(factor), in_slot_order(partner_factor)]

    starts = [group * height, (group ^ 1) * height]

    def of_rows(values):
        table = values.reshape(rows_here, BLK)
        return [lax.dynamic_slice_in_dim(table, start, height, 1) for start in starts]

    scales, spreads = of_rows(capacity), of_rows(spread)
    maps = of_rows(lax.dynamic_slice_in_dim(bus_map, own * rows_here * BLK, rows_here * BLK, 0))
    bus_ids = jnp.arange(buses, dtype=jnp.int32)
    onehots = [
        (m.reshape(-1)[None, :] == bus_ids[:, None]).astype(jnp.bfloat16) for m in maps
    ]

    arrivals = []
    for part in parts:
        outgoing = part.reshape(block_count, BLK, width)[block_index]
        if arrivals:
            outgoing, arrivals[-1] = lax.optimization_barrier((outgoing, arrivals[-1]))
        arrivals.append(
            lax.all_to_all(outgoing, "site", split_axis=0, concat_axis=0, tiled=True)
        )

    totals = []
    for arrived in arrivals:
        blocks = arrived.reshape(slots, BLK, width)
        total = None
        for portion, scale, deviation, onehot in zip(ordered, scales, spreads, onehots):
            spatial = jnp.einsum(
                "ksij,sjw->kiw", portion, blocks, preferred_element_type=jnp.float32
            ).astype(jnp.bfloat16)
            hourly = spatial.reshape(rows_here, height, scen_here, HOURS)
            weather = jnp.einsum(
                "kpsg,hg->kpsh", hourly, temporal, preferred_element_type=jnp.float32
            )
            scale_part = scale[:, :, None, None]
            spread_part = deviation[:, :, None, None]
            values = scale_part * jnp.exp(spread_part * weather - 0.5 * spread_part * spread_part)
            injected = values.astype(jnp.bfloat16).reshape(rows_here * height, width)
            term = jnp.dot(onehot, injected, preferred_element_type=jnp.float32)
            total = term if total is None else total + term
        totals.append(total)

    stacked = jnp.concatenate(totals, axis=1).reshape(sites, buses // sites, -1)
    shares = lax.all_to_all(stacked, "site", split_axis=0, concat_axis=0, tiled=True)
    mine = jnp.sum(shares, axis=0)
    result = mine[:, :width]
    for s in range(1, halves):
        back = [(z, (z - 2 * s) % groups) for z in range(groups)]
        result = result + lax.ppermute(mine[:, s * width : (s + 1) * width], "scen", back)
    return result


def solution(mesh):
    placed = (P("site", "scen"), P(), P("site", None, "scen", None), P(), P("site"), P("site"), P())
    sites = mesh.shape["site"]

    def whole(normals, pattern, factor, temporal, capacity, spread, bus_map):
        buses = sites * (factor.shape[0] // sites) * BLK // 16
        body = lambda *args: shards(*args, buses)
        return jax.shard_map(
            body, mesh=mesh, in_specs=placed, out_specs=P("site", "scen"), check_vma=False
        )(normals, pattern, factor, temporal, capacity, spread, bus_map)

    return whole
```

```python
import jax
import jax.numpy as jnp
from jax import lax
from jax.sharding import PartitionSpec as P

BLK = 256
HOURS = 168
NZ = 40
MAX_COLUMN_BLOCKS = 5
CHUNKS = 2


def shards(normals, pattern, factor, temporal, capacity, spread, bus_map, buses):
    own = lax.axis_index("site")
    sites = lax.axis_size("site")
    group = lax.axis_index("scen")
    groups = lax.axis_size("scen")
    width = normals.shape[1]
    scen_here = width // HOURS
    rows_here, _, height, _ = factor.shape
    halves = groups // 2

    parts = [normals]
    for s in range(1, halves):
        moved = [(z, (z + 2 * s) % groups) for z in range(groups)]
        parts.append(lax.ppermute(normals, "scen", moved))
    step = rows_here // CHUNKS
    partner_chunks = []
    for c in range(CHUNKS):
        piece = factor[c * step : (c + 1) * step]
        swap = [(z, z ^ 1) for z in range(groups)]
        partner_chunks.append(lax.ppermute(piece, "scen", swap))

    block_count = normals.shape[0] // BLK
    all_blocks = block_count * sites
    block_ids = jnp.arange(all_blocks, dtype=jnp.int32)
    wanted = pattern.reshape(sites, -1)
    needed = jnp.any(wanted[:, :, None] == block_ids[None, None, :], axis=1)
    owned_need = lax.dynamic_slice_in_dim(needed, own * block_count, block_count, 1)
    owned_need = owned_need.astype(jnp.int32)
    slot_rank = jnp.cumsum(owned_need, axis=1) - 1
    slot_ids = jnp.arange(MAX_COLUMN_BLOCKS, dtype=jnp.int32)
    chosen = (owned_need[:, None, :] == 1) & (slot_rank[:, None, :] == slot_ids[None, :, None])
    local_ids = jnp.arange(block_count, dtype=jnp.int32)
    block_index = jnp.sum(jnp.where(chosen, local_ids[None, None, :], 0), axis=2)

    my_columns = lax.dynamic_slice_in_dim(pattern, own * rows_here, rows_here, 0)
    my_need = lax.dynamic_index_in_dim(needed, own, 0, keepdims=False).astype(jnp.int32)
    my_rank = (jnp.cumsum(my_need.reshape(sites, block_count), axis=1) - 1).reshape(-1)
    slot_of_block = block_ids // block_count * MAX_COLUMN_BLOCKS + my_rank
    slots = sites * MAX_COLUMN_BLOCKS
    slot_of = jnp.sum(
        jnp.where(my_columns[:, :, None] == block_ids, slot_of_block[None, None, :], 0), axis=2
    )
    match = slot_of[:, None, :] == jnp.arange(slots, dtype=jnp.int32)[None, :, None]
    place = jnp.sum(jnp.where(match, jnp.arange(NZ, dtype=jnp.int32), 0), axis=2)
    named = jnp.any(match, axis=2)

    def in_slot_order(blocks, first):
        count = blocks.shape[0]
        flat = blocks.reshape(count * NZ, height, BLK)
        rows = jnp.arange(count, dtype=jnp.int32)[:, None]
        ordered = flat[place[first : first + count] + rows * NZ]
        if slots > NZ:
            keep = named[first : first + count, :, None, None]
            ordered = jnp.where(keep, ordered, jnp.zeros((), flat.dtype))
        return ordered

    pieces = [(in_slot_order(factor, 0), 0, 0)]
    for c, chunk in enumerate(partner_chunks):
        pieces.append((in_slot_order(chunk, c * step), c * step, 1))

    starts = [group * height, (group ^ 1) * height]

    def of_rows(values):
        table = values.reshape(rows_here, BLK)
        return [lax.dynamic_slice_in_dim(table, start, height, 1) for start in starts]

    scales, spreads = of_rows(capacity), of_rows(spread)
    maps = of_rows(lax.dynamic_slice_in_dim(bus_map, own * rows_here * BLK, rows_here * BLK, 0))
    bus_ids = jnp.arange(buses, dtype=jnp.int32)

    arrivals = []
    for part in parts:
        blocks = part.T.reshape(width, block_count, BLK).transpose(1, 0, 2)
        outgoing = blocks[block_index]
        if arrivals:
            outgoing, arrivals[-1] = lax.optimization_barrier((outgoing, arrivals[-1]))
        arrivals.append(lax.all_to_all(outgoing, "site", split_axis=0, concat_axis=0, tiled=True))

    totals = []
    for arrived in arrivals:
        blocks = arrived.reshape(slots, width, BLK)
        total = None
        for portion, first, half in pieces:
            count = portion.shape[0]
            spatial = jnp.einsum(
                "ksij,swj->kiw", portion, blocks, preferred_element_type=jnp.float32
            ).astype(jnp.bfloat16)
            hourly = spatial.reshape(count, height, scen_here, HOURS)
            weather = jnp.einsum(
                "kpsg,hg->kpsh", hourly, temporal, preferred_element_type=jnp.float32
            )
            scale_part = scales[half][first : first + count, :, None, None]
            spread_part = spreads[half][first : first + count, :, None, None]
            values = scale_part * jnp.exp(spread_part * weather - 0.5 * spread_part * spread_part)
            injected = values.astype(jnp.bfloat16).reshape(count * height, width)
            here = maps[half][first : first + count].reshape(-1)
            onehot = (here[None, :] == bus_ids[:, None]).astype(jnp.bfloat16)
            term = jnp.dot(onehot, injected, preferred_element_type=jnp.float32)
            total = term if total is None else total + term
        totals.append(total.astype(jnp.bfloat16).reshape(sites, buses // sites, width))

    stacked = jnp.concatenate(totals, axis=2)
    shares = lax.all_to_all(stacked, "site", split_axis=0, concat_axis=0, tiled=True)
    mine = jnp.sum(shares.astype(jnp.float32), axis=0)
    result = mine[:, :width]
    for s in range(1, halves):
        back = [(z, (z - 2 * s) % groups) for z in range(groups)]
        result = result + lax.ppermute(mine[:, s * width : (s + 1) * width], "scen", back)
    return result


def solution(mesh):
    placed = (P("site", "scen"), P(), P("site", None, "scen", None), P(), P("site"), P("site"), P())
    sites = mesh.shape["site"]

    def whole(normals, pattern, factor, temporal, capacity, spread, bus_map):
        buses = sites * (factor.shape[0] // sites) * BLK // 16

        def body(*args):
            return shards(*args, buses)

        return jax.shard_map(
            body, mesh=mesh, in_specs=placed, out_specs=P("site", "scen"), check_vma=False
        )(normals, pattern, factor, temporal, capacity, spread, bus_map)

    return whole
```

```python
import jax
import jax.numpy as jnp
from jax import lax
from jax.experimental import pallas as pl
from jax.experimental.pallas import tpu as pltpu
from jax.sharding import PartitionSpec as P

BLK = 256
HOURS = 168
NZ = 40
MAX_COLUMN_BLOCKS = 5
CHUNKS = 1


def pick_body(index_ref, table_ref, out_ref):
    row = pl.program_id(0)
    for slot in range(MAX_COLUMN_BLOCKS):
        start = pl.multiple_of(index_ref[row, slot] * BLK, BLK)
        out_ref[0, slot] = table_ref[:, pl.ds(start, BLK)]


def pick(index, table):
    sites, slots = index.shape
    width, lanes = table.shape
    return pl.pallas_call(
        pick_body,
        grid_spec=pltpu.PrefetchScalarGridSpec(
            num_scalar_prefetch=1,
            grid=(sites,),
            in_specs=[pl.BlockSpec((width, lanes), lambda i, index_ref: (0, 0))],
            out_specs=pl.BlockSpec((1, slots, width, BLK), lambda i, index_ref: (i, 0, 0, 0)),
        ),
        out_shape=jax.ShapeDtypeStruct((sites, slots, width, BLK), table.dtype),
        cost_estimate=pl.CostEstimate(
            flops=0, bytes_accessed=2 * sites * slots * width * BLK * 2, transcendentals=0
        ),
    )(index, table)


def shards(normals, pattern, factor, temporal, capacity, spread, bus_map, buses):
    own = lax.axis_index("site")
    sites = lax.axis_size("site")
    group = lax.axis_index("scen")
    groups = lax.axis_size("scen")
    width = normals.shape[1]
    scen_here = width // HOURS
    rows_here, _, height, _ = factor.shape
    halves = groups // 2

    parts = [normals]
    for s in range(1, halves):
        moved = [(z, (z + 2 * s) % groups) for z in range(groups)]
        parts.append(lax.ppermute(normals, "scen", moved))
    step = rows_here // CHUNKS
    partner_chunks = []
    for c in range(CHUNKS):
        piece = factor[c * step : (c + 1) * step] if CHUNKS > 1 else factor
        swap = [(z, z ^ 1) for z in range(groups)]
        partner_chunks.append(lax.ppermute(piece, "scen", swap))

    block_count = normals.shape[0] // BLK
    all_blocks = block_count * sites
    block_ids = jnp.arange(all_blocks, dtype=jnp.int32)
    wanted = pattern.reshape(sites, -1)
    needed = jnp.any(wanted[:, :, None] == block_ids[None, None, :], axis=1)
    owned_need = lax.dynamic_slice_in_dim(needed, own * block_count, block_count, 1)
    owned_need = owned_need.astype(jnp.int32)
    slot_rank = jnp.cumsum(owned_need, axis=1) - 1
    slot_ids = jnp.arange(MAX_COLUMN_BLOCKS, dtype=jnp.int32)
    chosen = (owned_need[:, None, :] == 1) & (slot_rank[:, None, :] == slot_ids[None, :, None])
    local_ids = jnp.arange(block_count, dtype=jnp.int32)
    block_index = jnp.sum(jnp.where(chosen, local_ids[None, None, :], 0), axis=2)

    my_columns = lax.dynamic_slice_in_dim(pattern, own * rows_here, rows_here, 0)
    my_need = lax.dynamic_index_in_dim(needed, own, 0, keepdims=False).astype(jnp.int32)
    my_rank = (jnp.cumsum(my_need.reshape(sites, block_count), axis=1) - 1).reshape(-1)
    slot_of_block = block_ids // block_count * MAX_COLUMN_BLOCKS + my_rank
    slots = sites * MAX_COLUMN_BLOCKS
    slot_of = jnp.sum(
        jnp.where(my_columns[:, :, None] == block_ids, slot_of_block[None, None, :], 0), axis=2
    )
    match = slot_of[:, None, :] == jnp.arange(slots, dtype=jnp.int32)[None, :, None]
    place = jnp.sum(jnp.where(match, jnp.arange(NZ, dtype=jnp.int32), 0), axis=2)
    named = jnp.any(match, axis=2)

    def in_slot_order(blocks, first):
        count = blocks.shape[0]
        flat = blocks.reshape(count * NZ, height, BLK)
        rows = jnp.arange(count, dtype=jnp.int32)[:, None]
        ordered = flat[place[first : first + count] + rows * NZ]
        if slots > NZ:
            keep = named[first : first + count, :, None, None]
            ordered = jnp.where(keep, ordered, jnp.zeros((), flat.dtype))
        return ordered

    pieces = [(in_slot_order(factor, 0), 0, 0)]
    for c, chunk in enumerate(partner_chunks):
        pieces.append((in_slot_order(chunk, c * step), c * step, 1))

    starts = [group * height, (group ^ 1) * height]

    def of_rows(values):
        table = values.reshape(rows_here, BLK)
        return [lax.dynamic_slice_in_dim(table, start, height, 1) for start in starts]

    scales, spreads = of_rows(capacity), of_rows(spread)
    maps = of_rows(lax.dynamic_slice_in_dim(bus_map, own * rows_here * BLK, rows_here * BLK, 0))
    bus_ids = jnp.arange(buses, dtype=jnp.int32)

    arrivals = []
    for part in parts:
        outgoing = pick(block_index, part.T)
        if arrivals:
            outgoing, arrivals[-1] = lax.optimization_barrier((outgoing, arrivals[-1]))
        arrivals.append(lax.all_to_all(outgoing, "site", split_axis=0, concat_axis=0, tiled=True))

    totals = []
    for arrived in arrivals:
        blocks = arrived.reshape(slots, width, BLK)
        total = None
        for portion, first, half in pieces:
            count = portion.shape[0]
            spatial = jnp.einsum(
                "ksij,swj->kiw", portion, blocks, preferred_element_type=jnp.float32
            ).astype(jnp.bfloat16)
            hourly = spatial.reshape(count, height, scen_here, HOURS)
            weather = jnp.einsum(
                "kpsg,hg->kpsh", hourly, temporal, preferred_element_type=jnp.float32
            )
            scale_part = scales[half][first : first + count, :, None, None]
            spread_part = spreads[half][first : first + count, :, None, None]
            values = scale_part * jnp.exp(spread_part * weather - 0.5 * spread_part * spread_part)
            injected = values.astype(jnp.bfloat16).reshape(count * height, width)
            here = maps[half][first : first + count].reshape(-1)
            onehot = (here[None, :] == bus_ids[:, None]).astype(jnp.bfloat16)
            term = jnp.dot(onehot, injected, preferred_element_type=jnp.float32)
            total = term if total is None else total + term
        totals.append(total.astype(jnp.bfloat16).reshape(sites, buses // sites, width))

    stacked = jnp.concatenate(totals, axis=2)
    shares = lax.all_to_all(stacked, "site", split_axis=0, concat_axis=0, tiled=True)
    mine = jnp.sum(shares.astype(jnp.float32), axis=0)
    result = mine[:, :width]
    for s in range(1, halves):
        back = [(z, (z - 2 * s) % groups) for z in range(groups)]
        result = result + lax.ppermute(mine[:, s * width : (s + 1) * width], "scen", back)
    return result


def solution(mesh):
    placed = (P("site", "scen"), P(), P("site", None, "scen", None), P(), P("site"), P("site"), P())
    sites = mesh.shape["site"]

    def whole(normals, pattern, factor, temporal, capacity, spread, bus_map):
        buses = sites * (factor.shape[0] // sites) * BLK // 16

        def body(*args):
            return shards(*args, buses)

        return jax.shard_map(
            body, mesh=mesh, in_specs=placed, out_specs=P("site", "scen"), check_vma=False
        )(normals, pattern, factor, temporal, capacity, spread, bus_map)

    return whole
```

```python
import jax
import jax.numpy as jnp
from jax import lax
from jax.experimental import pallas as pl
from jax.experimental.pallas import tpu as pltpu
from jax.sharding import PartitionSpec as P

BLK = 256
HOURS = 168
NZ = 40
MAX_COLUMN_BLOCKS = 5
CHUNKS = 1


def pick_body(index_ref, table_ref, out_ref):
    row = pl.program_id(0)
    for slot in range(MAX_COLUMN_BLOCKS):
        start = pl.multiple_of(index_ref[row, slot] * BLK, BLK)
        out_ref[0, slot] = table_ref[:, pl.ds(start, BLK)]


def pick(index, table):
    sites, slots = index.shape
    width, lanes = table.shape
    return pl.pallas_call(
        pick_body,
        grid_spec=pltpu.PrefetchScalarGridSpec(
            num_scalar_prefetch=1,
            grid=(sites,),
            in_specs=[pl.BlockSpec((width, lanes), lambda i, index_ref: (0, 0))],
            out_specs=pl.BlockSpec((1, slots, width, BLK), lambda i, index_ref: (i, 0, 0, 0)),
        ),
        out_shape=jax.ShapeDtypeStruct((sites, slots, width, BLK), table.dtype),
        cost_estimate=pl.CostEstimate(
            flops=0, bytes_accessed=2 * sites * slots * width * BLK * 2, transcendentals=0
        ),
    )(index, table)


def shards(normals, pattern, factor, temporal, capacity, spread, bus_map, buses):
    own = lax.axis_index("site")
    sites = lax.axis_size("site")
    group = lax.axis_index("scen")
    groups = lax.axis_size("scen")
    width = normals.shape[1]
    scen_here = width // HOURS
    rows_here, _, height, _ = factor.shape
    halves = groups // 2

    parts = [normals]
    for s in range(1, halves):
        moved = [(z, (z + 2 * s) % groups) for z in range(groups)]
        parts.append(lax.ppermute(normals, "scen", moved))
    step = rows_here // CHUNKS
    partner_chunks = []
    for c in range(CHUNKS):
        piece = factor[c * step : (c + 1) * step] if CHUNKS > 1 else factor
        swap = [(z, z ^ 1) for z in range(groups)]
        partner_chunks.append(lax.ppermute(piece, "scen", swap))

    block_count = normals.shape[0] // BLK
    all_blocks = block_count * sites
    block_ids = jnp.arange(all_blocks, dtype=jnp.int32)
    wanted = pattern.reshape(sites, -1)
    needed = jnp.any(wanted[:, :, None] == block_ids[None, None, :], axis=1)
    owned_need = lax.dynamic_slice_in_dim(needed, own * block_count, block_count, 1)
    owned_need = owned_need.astype(jnp.int32)
    slot_rank = jnp.cumsum(owned_need, axis=1) - 1
    slot_ids = jnp.arange(MAX_COLUMN_BLOCKS, dtype=jnp.int32)
    chosen = (owned_need[:, None, :] == 1) & (slot_rank[:, None, :] == slot_ids[None, :, None])
    local_ids = jnp.arange(block_count, dtype=jnp.int32)
    block_index = jnp.sum(jnp.where(chosen, local_ids[None, None, :], 0), axis=2)

    my_columns = lax.dynamic_slice_in_dim(pattern, own * rows_here, rows_here, 0)
    my_need = lax.dynamic_index_in_dim(needed, own, 0, keepdims=False).astype(jnp.int32)
    my_rank = (jnp.cumsum(my_need.reshape(sites, block_count), axis=1) - 1).reshape(-1)
    slot_of_block = block_ids // block_count * MAX_COLUMN_BLOCKS + my_rank
    slots = sites * MAX_COLUMN_BLOCKS
    slot_of = jnp.sum(
        jnp.where(my_columns[:, :, None] == block_ids, slot_of_block[None, None, :], 0), axis=2
    )
    match = slot_of[:, None, :] == jnp.arange(slots, dtype=jnp.int32)[None, :, None]
    place = jnp.sum(jnp.where(match, jnp.arange(NZ, dtype=jnp.int32), 0), axis=2)
    named = jnp.any(match, axis=2)

    def in_slot_order(blocks, first):
        count = blocks.shape[0]
        flat = blocks.reshape(count * NZ, height, BLK)
        rows = jnp.arange(count, dtype=jnp.int32)[:, None]
        ordered = flat[place[first : first + count] + rows * NZ]
        if slots > NZ:
            keep = named[first : first + count, :, None, None]
            ordered = jnp.where(keep, ordered, jnp.zeros((), flat.dtype))
        return ordered

    pieces = [(in_slot_order(factor, 0), 0, 0)]
    for c, chunk in enumerate(partner_chunks):
        pieces.append((in_slot_order(chunk, c * step), c * step, 1))

    starts = [group * height, (group ^ 1) * height]

    def of_rows(values):
        table = values.reshape(rows_here, BLK)
        return [lax.dynamic_slice_in_dim(table, start, height, 1) for start in starts]

    scales, spreads = of_rows(capacity), of_rows(spread)
    maps = of_rows(lax.dynamic_slice_in_dim(bus_map, own * rows_here * BLK, rows_here * BLK, 0))
    bus_ids = jnp.arange(buses, dtype=jnp.int32)

    arrivals = []
    for part in parts:
        outgoing = pick(block_index, part.T)
        if arrivals:
            outgoing, arrivals[-1] = lax.optimization_barrier((outgoing, arrivals[-1]))
        arrivals.append(lax.all_to_all(outgoing, "site", split_axis=0, concat_axis=0, tiled=True))

    totals = []
    for arrived in arrivals:
        blocks = arrived.reshape(slots, width, BLK)
        total = None
        for portion, first, half in pieces:
            count = portion.shape[0]
            spatial = jnp.einsum(
                "ksij,swj->kiw", portion, blocks, preferred_element_type=jnp.float32
            ).astype(jnp.bfloat16)
            hourly = spatial.reshape(count, height, scen_here, HOURS)
            weather = jnp.einsum(
                "kpsg,hg->kpsh", hourly, temporal, preferred_element_type=jnp.float32
            )
            scale_part = scales[half][first : first + count, :, None, None]
            spread_part = spreads[half][first : first + count, :, None, None]
            values = scale_part * jnp.exp(spread_part * weather - 0.5 * spread_part * spread_part)
            injected = values.astype(jnp.bfloat16).reshape(count * height, width)
            here = maps[half][first : first + count].reshape(-1)
            onehot = (here[None, :] == bus_ids[:, None]).astype(jnp.bfloat16)
            term = jnp.dot(onehot, injected, preferred_element_type=jnp.float32)
            total = term if total is None else total + term
        totals.append(total.astype(jnp.bfloat16).reshape(sites, buses // sites, width))

    order = jnp.mod(group // 2 - jnp.arange(halves, dtype=jnp.int32), halves)
    stacked = jnp.stack(totals, axis=1)[:, order] if halves > 2 else jnp.where(
        group // 2 == 0, jnp.stack(totals, axis=1), jnp.stack(totals[::-1], axis=1)
    )
    stacked = stacked.reshape(sites * halves, buses // sites, width)
    members = [
        [k * groups + 2 * h + parity for k in range(sites) for h in range(halves)]
        for parity in range(2)
    ]
    shares = lax.all_to_all(
        stacked,
        ("site", "scen"),
        split_axis=0,
        concat_axis=0,
        axis_index_groups=members,
        tiled=True,
    )
    return jnp.sum(shares.astype(jnp.float32), axis=0)


def solution(mesh):
    placed = (P("site", "scen"), P(), P("site", None, "scen", None), P(), P("site"), P("site"), P())
    sites = mesh.shape["site"]

    def whole(normals, pattern, factor, temporal, capacity, spread, bus_map):
        buses = sites * (factor.shape[0] // sites) * BLK // 16

        def body(*args):
            return shards(*args, buses)

        return jax.shard_map(
            body, mesh=mesh, in_specs=placed, out_specs=P("site", "scen"), check_vma=False
        )(normals, pattern, factor, temporal, capacity, spread, bus_map)

    return whole
```

```python
import functools

import jax
import jax.numpy as jnp
from jax import lax
from jax.experimental import pallas as pl
from jax.experimental.pallas import tpu as pltpu
from jax.sharding import PartitionSpec as P

BLK = 256
HOURS = 168
NZ = 40
MAX_COLUMN_BLOCKS = 5
CHUNKS = 1


def pick_body(index_ref, table_ref, out_ref):
    row = pl.program_id(0)
    for slot in range(MAX_COLUMN_BLOCKS):
        start = pl.multiple_of(index_ref[row, slot] * BLK, BLK)
        out_ref[0, slot] = table_ref[:, pl.ds(start, BLK)]


def pick(index, table):
    sites, slots = index.shape
    width, lanes = table.shape
    return pl.pallas_call(
        pick_body,
        grid_spec=pltpu.PrefetchScalarGridSpec(
            num_scalar_prefetch=1,
            grid=(sites,),
            in_specs=[pl.BlockSpec((width, lanes), lambda i, index_ref: (0, 0))],
            out_specs=pl.BlockSpec((1, slots, width, BLK), lambda i, index_ref: (i, 0, 0, 0)),
        ),
        out_shape=jax.ShapeDtypeStruct((sites, slots, width, BLK), table.dtype),
        cost_estimate=pl.CostEstimate(
            flops=0, bytes_accessed=2 * sites * slots * width * BLK * 2, transcendentals=0
        ),
    )(index, table)


def exchange_body(sites, groups, *refs):
    halves = groups // 2
    share_refs = refs[:halves]
    out_ref, landed, send_sem, recv_sem = refs[halves:]
    own = lax.axis_index("site")
    group = lax.axis_index("scen")
    offsets = [(a, h) for a in range(sites) for h in range(halves)][1:]
    peers = [
        (lax.rem(own + a, sites), lax.rem(group + 2 * h, groups)) for a, h in offsets
    ]
    barrier = pltpu.get_barrier_semaphore()
    for peer in peers:
        pl.semaphore_signal(
            barrier, inc=1, device_id=peer, device_id_type=pl.DeviceIdType.MESH
        )
    pl.semaphore_wait(barrier, len(peers))
    copies = []
    for n, ((_, h), peer) in enumerate(zip(offsets, peers)):
        copies.append(
            pltpu.make_async_remote_copy(
                src_ref=share_refs[(halves - h) % halves].at[peer[0]],
                dst_ref=landed.at[n],
                send_sem=send_sem.at[n],
                recv_sem=recv_sem.at[n],
                device_id=peer,
                device_id_type=pl.DeviceIdType.MESH,
            )
        )
        copies[-1].start()
    total = share_refs[0][own].astype(jnp.float32)
    for n, copy in enumerate(copies):
        copy.wait_recv()
        total = total + landed[n].astype(jnp.float32)
    for copy in copies:
        copy.wait_send()
    out_ref[...] = total


def exchange(shares, sites, groups):
    _, height, width = shares[0].shape
    count = sites * len(shares) - 1
    return pl.pallas_call(
        functools.partial(exchange_body, sites, groups),
        out_shape=jax.ShapeDtypeStruct((height, width), jnp.float32),
        in_specs=[pl.BlockSpec(memory_space=pltpu.VMEM)] * len(shares),
        out_specs=pl.BlockSpec(memory_space=pltpu.VMEM),
        scratch_shapes=[
            pltpu.VMEM((count, height, width), shares[0].dtype),
            pltpu.SemaphoreType.DMA((count,)),
            pltpu.SemaphoreType.DMA((count,)),
        ],
        compiler_params=pltpu.CompilerParams(collective_id=0, has_side_effects=True),
    )(*shares)


def shards(normals, pattern, factor, temporal, capacity, spread, bus_map, buses):
    own = lax.axis_index("site")
    sites = lax.axis_size("site")
    group = lax.axis_index("scen")
    groups = lax.axis_size("scen")
    width = normals.shape[1]
    scen_here = width // HOURS
    rows_here, _, height, _ = factor.shape
    halves = groups // 2

    parts = [normals]
    for s in range(1, halves):
        moved = [(z, (z + 2 * s) % groups) for z in range(groups)]
        parts.append(lax.ppermute(normals, "scen", moved))
    step = rows_here // CHUNKS
    partner_chunks = []
    for c in range(CHUNKS):
        piece = factor[c * step : (c + 1) * step] if CHUNKS > 1 else factor
        swap = [(z, z ^ 1) for z in range(groups)]
        partner_chunks.append(lax.ppermute(piece, "scen", swap))

    block_count = normals.shape[0] // BLK
    all_blocks = block_count * sites
    block_ids = jnp.arange(all_blocks, dtype=jnp.int32)
    wanted = pattern.reshape(sites, -1)
    needed = jnp.any(wanted[:, :, None] == block_ids[None, None, :], axis=1)
    owned_need = lax.dynamic_slice_in_dim(needed, own * block_count, block_count, 1)
    owned_need = owned_need.astype(jnp.int32)
    slot_rank = jnp.cumsum(owned_need, axis=1) - 1
    slot_ids = jnp.arange(MAX_COLUMN_BLOCKS, dtype=jnp.int32)
    chosen = (owned_need[:, None, :] == 1) & (slot_rank[:, None, :] == slot_ids[None, :, None])
    local_ids = jnp.arange(block_count, dtype=jnp.int32)
    block_index = jnp.sum(jnp.where(chosen, local_ids[None, None, :], 0), axis=2)

    my_columns = lax.dynamic_slice_in_dim(pattern, own * rows_here, rows_here, 0)
    my_need = lax.dynamic_index_in_dim(needed, own, 0, keepdims=False).astype(jnp.int32)
    my_rank = (jnp.cumsum(my_need.reshape(sites, block_count), axis=1) - 1).reshape(-1)
    slot_of_block = block_ids // block_count * MAX_COLUMN_BLOCKS + my_rank
    slots = sites * MAX_COLUMN_BLOCKS
    slot_of = jnp.sum(
        jnp.where(my_columns[:, :, None] == block_ids, slot_of_block[None, None, :], 0), axis=2
    )
    match = slot_of[:, None, :] == jnp.arange(slots, dtype=jnp.int32)[None, :, None]
    place = jnp.sum(jnp.where(match, jnp.arange(NZ, dtype=jnp.int32), 0), axis=2)
    named = jnp.any(match, axis=2)

    def in_slot_order(blocks, first):
        count = blocks.shape[0]
        flat = blocks.reshape(count * NZ, height, BLK)
        rows = jnp.arange(count, dtype=jnp.int32)[:, None]
        ordered = flat[place[first : first + count] + rows * NZ]
        if slots > NZ:
            keep = named[first : first + count, :, None, None]
            ordered = jnp.where(keep, ordered, jnp.zeros((), flat.dtype))
        return ordered

    pieces = [(in_slot_order(factor, 0), 0, 0)]
    for c, chunk in enumerate(partner_chunks):
        pieces.append((in_slot_order(chunk, c * step), c * step, 1))

    starts = [group * height, (group ^ 1) * height]

    def of_rows(values):
        table = values.reshape(rows_here, BLK)
        return [lax.dynamic_slice_in_dim(table, start, height, 1) for start in starts]

    scales, spreads = of_rows(capacity), of_rows(spread)
    maps = of_rows(lax.dynamic_slice_in_dim(bus_map, own * rows_here * BLK, rows_here * BLK, 0))
    bus_ids = jnp.arange(buses, dtype=jnp.int32)

    arrivals = []
    for part in parts:
        outgoing = pick(block_index, part.T)
        if arrivals:
            outgoing, arrivals[-1] = lax.optimization_barrier((outgoing, arrivals[-1]))
        arrivals.append(lax.all_to_all(outgoing, "site", split_axis=0, concat_axis=0, tiled=True))

    totals = []
    for arrived in arrivals:
        blocks = arrived.reshape(slots, width, BLK)
        total = None
        for portion, first, half in pieces:
            count = portion.shape[0]
            spatial = jnp.einsum(
                "ksij,swj->kiw", portion, blocks, preferred_element_type=jnp.float32
            ).astype(jnp.bfloat16)
            hourly = spatial.reshape(count, height, scen_here, HOURS)
            weather = jnp.einsum(
                "kpsg,hg->kpsh", hourly, temporal, preferred_element_type=jnp.float32
            )
            scale_part = scales[half][first : first + count, :, None, None]
            spread_part = spreads[half][first : first + count, :, None, None]
            values = scale_part * jnp.exp(spread_part * weather - 0.5 * spread_part * spread_part)
            injected = values.astype(jnp.bfloat16).reshape(count * height, width)
            here = maps[half][first : first + count].reshape(-1)
            onehot = (here[None, :] == bus_ids[:, None]).astype(jnp.bfloat16)
            term = jnp.dot(onehot, injected, preferred_element_type=jnp.float32)
            total = term if total is None else total + term
        totals.append(total.astype(jnp.bfloat16).reshape(sites, buses // sites, width))

    return exchange(totals, sites, groups)


def solution(mesh):
    placed = (P("site", "scen"), P(), P("site", None, "scen", None), P(), P("site"), P("site"), P())
    sites = mesh.shape["site"]

    def whole(normals, pattern, factor, temporal, capacity, spread, bus_map):
        buses = sites * (factor.shape[0] // sites) * BLK // 16

        def body(*args):
            return shards(*args, buses)

        return jax.shard_map(
            body, mesh=mesh, in_specs=placed, out_specs=P("site", "scen"), check_vma=False
        )(normals, pattern, factor, temporal, capacity, spread, bus_map)

    return whole
```

```python
import functools

import jax
import jax.numpy as jnp
from jax import lax
from jax.experimental import pallas as pl
from jax.experimental.pallas import tpu as pltpu
from jax.sharding import PartitionSpec as P

BLK = 256
HOURS = 168
NZ = 40
MAX_COLUMN_BLOCKS = 5
CHUNKS = 1


def pick_body(index_ref, table_ref, out_ref):
    row = pl.program_id(0)
    for slot in range(MAX_COLUMN_BLOCKS):
        start = pl.multiple_of(index_ref[row, slot] * BLK, BLK)
        out_ref[0, slot] = table_ref[:, pl.ds(start, BLK)]


def pick(index, table):
    sites, slots = index.shape
    width, lanes = table.shape
    return pl.pallas_call(
        pick_body,
        grid_spec=pltpu.PrefetchScalarGridSpec(
            num_scalar_prefetch=1,
            grid=(sites,),
            in_specs=[pl.BlockSpec((width, lanes), lambda i, index_ref: (0, 0))],
            out_specs=pl.BlockSpec((1, slots, width, BLK), lambda i, index_ref: (i, 0, 0, 0)),
        ),
        out_shape=jax.ShapeDtypeStruct((sites, slots, width, BLK), table.dtype),
        cost_estimate=pl.CostEstimate(
            flops=0, bytes_accessed=2 * sites * slots * width * BLK * 2, transcendentals=0
        ),
    )(index, table)


def exchange_body(sites, groups, *refs):
    halves = groups // 2
    share_refs = refs[:halves]
    out_ref, landed, send_sem, recv_sem = refs[halves:]
    own = lax.axis_index("site")
    group = lax.axis_index("scen")
    peers = [(lax.rem(own + a, sites), group) for a in range(1, sites)]
    barrier = pltpu.get_barrier_semaphore()
    for peer in peers:
        pl.semaphore_signal(
            barrier, inc=1, device_id=peer, device_id_type=pl.DeviceIdType.MESH
        )
    pl.semaphore_wait(barrier, len(peers))
    copies = []
    for h in range(halves):
        for n, peer in enumerate(peers):
            copies.append(
                pltpu.make_async_remote_copy(
                    src_ref=share_refs[h].at[peer[0]],
                    dst_ref=landed.at[h, n],
                    send_sem=send_sem.at[h, n],
                    recv_sem=recv_sem.at[h, n],
                    device_id=peer,
                    device_id_type=pl.DeviceIdType.MESH,
                )
            )
            copies[-1].start()
    for h in range(halves):
        total = share_refs[h][own].astype(jnp.float32)
        for n in range(len(peers)):
            copies[h * len(peers) + n].wait_recv()
            total = total + landed[h, n].astype(jnp.float32)
        out_ref[h] = total
    for copy in copies:
        copy.wait_send()


def exchange(shares, sites, groups):
    _, height, width = shares[0].shape
    slots = (len(shares), sites - 1)
    return pl.pallas_call(
        functools.partial(exchange_body, sites, groups),
        out_shape=jax.ShapeDtypeStruct((len(shares), height, width), jnp.float32),
        in_specs=[pl.BlockSpec(memory_space=pltpu.VMEM)] * len(shares),
        out_specs=pl.BlockSpec(memory_space=pltpu.VMEM),
        scratch_shapes=[
            pltpu.VMEM((*slots, height, width), shares[0].dtype),
            pltpu.SemaphoreType.DMA(slots),
            pltpu.SemaphoreType.DMA(slots),
        ],
        compiler_params=pltpu.CompilerParams(collective_id=0, has_side_effects=True),
    )(*shares)


def shards(normals, pattern, factor, temporal, capacity, spread, bus_map, buses):
    own = lax.axis_index("site")
    sites = lax.axis_size("site")
    group = lax.axis_index("scen")
    groups = lax.axis_size("scen")
    width = normals.shape[1]
    scen_here = width // HOURS
    rows_here, _, height, _ = factor.shape
    halves = groups // 2

    parts = [normals]
    for s in range(1, halves):
        moved = [(z, (z + 2 * s) % groups) for z in range(groups)]
        parts.append(lax.ppermute(normals, "scen", moved))
    step = rows_here // CHUNKS
    partner_chunks = []
    for c in range(CHUNKS):
        piece = factor[c * step : (c + 1) * step] if CHUNKS > 1 else factor
        swap = [(z, z ^ 1) for z in range(groups)]
        partner_chunks.append(lax.ppermute(piece, "scen", swap))

    block_count = normals.shape[0] // BLK
    all_blocks = block_count * sites
    block_ids = jnp.arange(all_blocks, dtype=jnp.int32)
    wanted = pattern.reshape(sites, -1)
    needed = jnp.any(wanted[:, :, None] == block_ids[None, None, :], axis=1)
    owned_need = lax.dynamic_slice_in_dim(needed, own * block_count, block_count, 1)
    owned_need = owned_need.astype(jnp.int32)
    slot_rank = jnp.cumsum(owned_need, axis=1) - 1
    slot_ids = jnp.arange(MAX_COLUMN_BLOCKS, dtype=jnp.int32)
    chosen = (owned_need[:, None, :] == 1) & (slot_rank[:, None, :] == slot_ids[None, :, None])
    local_ids = jnp.arange(block_count, dtype=jnp.int32)
    block_index = jnp.sum(jnp.where(chosen, local_ids[None, None, :], 0), axis=2)

    my_columns = lax.dynamic_slice_in_dim(pattern, own * rows_here, rows_here, 0)
    my_need = lax.dynamic_index_in_dim(needed, own, 0, keepdims=False).astype(jnp.int32)
    my_rank = (jnp.cumsum(my_need.reshape(sites, block_count), axis=1) - 1).reshape(-1)
    slot_of_block = block_ids // block_count * MAX_COLUMN_BLOCKS + my_rank
    slots = sites * MAX_COLUMN_BLOCKS
    slot_of = jnp.sum(
        jnp.where(my_columns[:, :, None] == block_ids, slot_of_block[None, None, :], 0), axis=2
    )
    match = slot_of[:, None, :] == jnp.arange(slots, dtype=jnp.int32)[None, :, None]
    place = jnp.sum(jnp.where(match, jnp.arange(NZ, dtype=jnp.int32), 0), axis=2)
    named = jnp.any(match, axis=2)

    def in_slot_order(blocks, first):
        count = blocks.shape[0]
        flat = blocks.reshape(count * NZ, height, BLK)
        rows = jnp.arange(count, dtype=jnp.int32)[:, None]
        ordered = flat[place[first : first + count] + rows * NZ]
        if slots > NZ:
            keep = named[first : first + count, :, None, None]
            ordered = jnp.where(keep, ordered, jnp.zeros((), flat.dtype))
        return ordered

    pieces = [(in_slot_order(factor, 0), 0, 0)]
    for c, chunk in enumerate(partner_chunks):
        pieces.append((in_slot_order(chunk, c * step), c * step, 1))

    starts = [group * height, (group ^ 1) * height]

    def of_rows(values):
        table = values.reshape(rows_here, BLK)
        return [lax.dynamic_slice_in_dim(table, start, height, 1) for start in starts]

    scales, spreads = of_rows(capacity), of_rows(spread)
    maps = of_rows(lax.dynamic_slice_in_dim(bus_map, own * rows_here * BLK, rows_here * BLK, 0))
    bus_ids = jnp.arange(buses, dtype=jnp.int32)

    arrivals = []
    for part in parts:
        outgoing = pick(block_index, part.T)
        if arrivals:
            outgoing, arrivals[-1] = lax.optimization_barrier((outgoing, arrivals[-1]))
        arrivals.append(lax.all_to_all(outgoing, "site", split_axis=0, concat_axis=0, tiled=True))

    totals = []
    for arrived in arrivals:
        blocks = arrived.reshape(slots, width, BLK)
        total = None
        for portion, first, half in pieces:
            count = portion.shape[0]
            spatial = jnp.einsum(
                "ksij,swj->kiw", portion, blocks, preferred_element_type=jnp.float32
            ).astype(jnp.bfloat16)
            hourly = spatial.reshape(count, height, scen_here, HOURS)
            weather = jnp.einsum(
                "kpsg,hg->kpsh", hourly, temporal, preferred_element_type=jnp.float32
            )
            scale_part = scales[half][first : first + count, :, None, None]
            spread_part = spreads[half][first : first + count, :, None, None]
            values = scale_part * jnp.exp(spread_part * weather - 0.5 * spread_part * spread_part)
            injected = values.astype(jnp.bfloat16).reshape(count * height, width)
            here = maps[half][first : first + count].reshape(-1)
            onehot = (here[None, :] == bus_ids[:, None]).astype(jnp.bfloat16)
            term = jnp.dot(onehot, injected, preferred_element_type=jnp.float32)
            total = term if total is None else total + term
        totals.append(total.astype(jnp.bfloat16).reshape(sites, buses // sites, width))

    mine = exchange(totals, sites, groups)
    result = mine[0]
    for s in range(1, halves):
        back = [(z, (z - 2 * s) % groups) for z in range(groups)]
        result = result + lax.ppermute(mine[s], "scen", back)
    return result


def solution(mesh):
    placed = (P("site", "scen"), P(), P("site", None, "scen", None), P(), P("site"), P("site"), P())
    sites = mesh.shape["site"]

    def whole(normals, pattern, factor, temporal, capacity, spread, bus_map):
        buses = sites * (factor.shape[0] // sites) * BLK // 16

        def body(*args):
            return shards(*args, buses)

        return jax.shard_map(
            body, mesh=mesh, in_specs=placed, out_specs=P("site", "scen"), check_vma=False
        )(normals, pattern, factor, temporal, capacity, spread, bus_map)

    return whole
```
